256 devices in a mesh: row: 8 (over z), col: 32 (over y, x, core).
Axes of the slice: x: 4, y: 4, z: 8, core: 2. Of those that a mesh axis runs over, the one named last changes fastest.
Arguments:
- covariance: float32 [8, 2048, 2, 8192], P(None, 'row', None, 'col'), may hold values from 0 to 16, as said below
Outputs:
- factor: float32 [8, 2048, 2, 8192], P(None, 'row', None, 'col')
The draws below stay inside these ranges and needn't reach their ends.
Inputs may be any that keep to these rules, and one draw needn't show every extreme that they name: Read as the matrix of order 16384, covariance is symmetric and positive definite.
All inputs are finite; a program needn't handle non-finite values.
Results may differ from the reference program's by a relative error of at most 0.000058.
Values sent between devices are 32-bit elements; how exact they have to be, the bound alone decides.
No kernel may reach another device: no remote copies, remote signals or barrier semaphores. Data moves between devices by JAX's collectives and lax.ppermute only.
A program may use at most 64 MiB of HBM per device.

```python
import math
import jax
import jax.numpy as jnp
from jax import lax

NB = 256
TIMES = 16
COL_TILES = 2
ROW_TILES = 8
ORDER = 16384
N_ROW = 8
N_COL = 32


def draw_covariance(key, part):
    matrix_order = ROW_TILES * N_ROW * NB
    site_count = matrix_order // TIMES
    key_place = jax.random.fold_in(key, 0)
    key_spread = jax.random.fold_in(key, 3)
    location = jax.random.uniform(key_place, (site_count, 2), dtype=jnp.float32)
    spread = jnp.exp(jax.random.uniform(key_spread, (matrix_order,), dtype=jnp.float32, minval=0.0, maxval=math.log(3.0)))
    offset_pair = location[:, None, :] - location[None, :, :]
    distance = jnp.sqrt(jnp.sum(offset_pair * offset_pair, axis=-1))
    moments = jnp.arange(TIMES, dtype=jnp.float32)
    stretch = 1.0 + 0.5 * jnp.abs(moments[:, None] - moments[None, :])
    kernel = jnp.exp(-distance[:, None, :, None] / (0.25 * jnp.sqrt(stretch)[None, :, None, :])) / stretch[None, :, None, :]
    kernel = kernel.reshape(matrix_order, matrix_order)
    points = jnp.arange(matrix_order)
    kernel = kernel + jnp.where(points[:, None] == points[None, :], 0.25, 0.0).astype(jnp.float32)
    result = spread[:, None] * spread[None, :] * kernel
    return result.reshape(ROW_TILES, N_ROW * NB, COL_TILES, N_COL * NB)


def setup_inputs(seed: int = 0) -> dict:
    key_of = jax.random.split(jax.random.key(seed), 2)
    return {
        "covariance": draw_covariance(jax.random.fold_in(key_of[1], 71), 0),
    }


def reference(covariance):
    matrix = covariance.reshape(ORDER, ORDER)
    chol_factor = jnp.linalg.cholesky(matrix[:NB, :NB])
    solved_panel = lax.linalg.triangular_solve(chol_factor, matrix[NB:, :NB], left_side=False, lower=True, transpose_a=True)
    trailing = matrix[NB:, NB:] - jnp.dot(solved_panel.astype(jnp.float32), solved_panel.T.astype(jnp.float32), precision=lax.Precision.HIGHEST, preferred_element_type=jnp.float32)
    top_rows = jnp.concatenate([chol_factor, solved_panel.T], axis=1)
    low_rows = jnp.concatenate([solved_panel, trailing], axis=1)
    factor = jnp.concatenate([top_rows, low_rows], axis=0)
    return factor.reshape(covariance.shape)
```

```python
import jax
import jax.numpy as jnp
from jax import lax
from jax.experimental import pallas as pl
from jax.experimental.pallas import tpu as pltpu
from jax.sharding import PartitionSpec as P

HI = lax.Precision.HIGHEST


def dot(a, b, ca=1, cb=0, precision=HI):
    return lax.dot_general(a, b, (((ca,), (cb,)), ((), ())), precision=precision, preferred_element_type=jnp.float32)


def factor_block(block):
    n = block.shape[0]
    rows = lax.broadcasted_iota(jnp.int32, (n, n), 0)
    cols = lax.broadcasted_iota(jnp.int32, (n, n), 1)
    sub = lax.broadcasted_iota(jnp.int32, (8, n), 0)
    left = block
    right = jnp.where(rows == cols, 1.0, 0.0).astype(jnp.float32)
    upper, inverse = [], []
    for g in range(n // 8):
        size = n - 8 * g
        for k in range(0, 8, 2):
            j = 8 * g + k
            c1 = jnp.broadcast_to(left[:, j:j + 1], (size, n))
            c2 = jnp.broadcast_to(left[:, j + 1:j + 2], (size, n))
            row1, row2 = left[k:k + 1, :], left[k + 1:k + 2, :]
            inv1, inv2 = right[k:k + 1, :], right[k + 1:k + 2, :]
            a = c1[k:k + 1]
            b = c2[k:k + 1]
            c = c2[k + 1:k + 2]
            ra = 1.0 / a
            m = b * ra
            d = c - b * m
            rd = 1.0 / d
            row2 = row2 - m * row1
            inv2 = inv2 - m * inv1
            v2, w2 = row2 * rd, inv2 * rd
            v1, w1 = row1 * ra - m * v2, inv1 * ra - m * w2
            sa, sd = lax.rsqrt(a), lax.rsqrt(d)
            upper += [row1 * sa, row2 * sd]
            inverse += [inv1 * sa, inv2 * sd]
            live = sub > k + 1
            t1 = jnp.where(live, c1[:8], 0.0)
            t2 = jnp.where(live, c2[:8], 0.0)
            if size > 8:
                c1 = jnp.concatenate([t1, c1[8:]], 0)
                c2 = jnp.concatenate([t2, c2[8:]], 0)
            else:
                c1, c2 = t1, t2
            left = left - c1 * v1 - c2 * v2
            right = right - c1 * w1 - c2 * w2
        left, right = left[8:], right[8:]
    upper = jnp.concatenate(upper, 0)
    inverse = jnp.concatenate(inverse, 0)
    return jnp.where(rows <= cols, upper, 0.0), inverse


def chol_kernel(a_ref, l_ref, inv_ref):
    h = a_ref.shape[0] // 2
    u0, y0 = factor_block(a_ref[:h, :h])
    l10 = dot(a_ref[h:, :h], y0, 1, 1)
    d1 = a_ref[h:, h:] - dot(l10, l10, 1, 1)
    u1, y1 = factor_block(d1)
    zero = jnp.zeros((h, h), jnp.float32)
    l_ref[:h, :h] = u0.T
    l_ref[:h, h:] = zero
    l_ref[h:, :h] = l10
    l_ref[h:, h:] = u1.T
    inv_ref[:h, :h] = y0
    inv_ref[:h, h:] = zero
    inv_ref[h:, :h] = -dot(y1, dot(l10, y0))
    inv_ref[h:, h:] = y1


def chol_inverse(a, **kw):
    s = jax.ShapeDtypeStruct(a.shape, jnp.float32)
    return pl.pallas_call(chol_kernel, out_shape=(s, s), name="chol", **kw)(a)


def final_kernel(info_ref, cov_ref, upper_ref, inv_ref, low_ref, *rest):
    tiles, out_ref = rest[:8], rest[8]
    cov_buf, tile_buf, cov_sem, tile_sem, out_sem = rest[9:]
    row, col = info_ref[8], info_ref[9]
    for j in range(8):
        pltpu.make_async_copy(cov_ref.at[info_ref[j]], cov_buf.at[j], cov_sem.at[j]).start()
        pltpu.make_async_copy(tiles[j], tile_buf.at[j], tile_sem.at[j]).start()
    inv = inv_ref[...]
    solved = [dot(inv, upper_ref[t]) for t in range(2)]
    weight = [dot(inv, solved[t], 0, 0) for t in range(2)]
    weight[0] = jnp.where(col == 0, -inv.T, weight[0])
    keep = [jnp.where(col == 0, 0.0, 1.0).astype(jnp.float32), None]
    for j in range(8):
        pltpu.make_async_copy(tiles[j], tile_buf.at[j], tile_sem.at[j]).wait()
        pltpu.make_async_copy(cov_ref.at[info_ref[j]], cov_buf.at[j], cov_sem.at[j]).wait()
        tile = tile_buf[j]
        for t in range(2):
            prod = dot(tile, weight[t])
            for q in range(2):
                part = pl.ds(2 * q + t, 256, stride=4)
                old = cov_buf[j, part, :]
                if t == 0:
                    old = old * keep[0]
                cov_buf[j, part, :] = old - prod[:, 128 * q:128 * q + 128]

        @pl.when((info_ref[j] == 0) & (row == 0))
        def _():
            for t in range(2):
                for q in range(2):
                    part = pl.ds(2 * q + t, 256, stride=4)
                    new = solved[t][:, 128 * q:128 * q + 128]
                    if t == 0:
                        new = jnp.where(col == 0, low_ref[:, 128 * q:128 * q + 128], new)
                    cov_buf[j, part, :] = new

        pltpu.make_async_copy(cov_buf.at[j], out_ref.at[info_ref[j]], out_sem.at[j]).start()
    for j in range(8):
        pltpu.make_async_copy(cov_buf.at[j], out_ref.at[info_ref[j]], out_sem.at[j]).wait()


def finish(info, cov, upper, inv, low, tiles):
    vmem = pl.BlockSpec(memory_space=pltpu.VMEM)
    hbm = pl.BlockSpec(memory_space=pl.ANY)
    return pl.pallas_call(
        final_kernel,
        out_shape=jax.ShapeDtypeStruct(cov.shape, jnp.float32),
        in_specs=[pl.BlockSpec(memory_space=pltpu.SMEM), hbm, vmem, vmem, vmem] + [hbm] * 8,
        out_specs=hbm,
        scratch_shapes=[
            pltpu.VMEM((8, 1024, 128), jnp.float32),
            pltpu.VMEM((8, 256, 256), jnp.float32),
            pltpu.SemaphoreType.DMA((8,)),
            pltpu.SemaphoreType.DMA((8,)),
            pltpu.SemaphoreType.DMA((8,)),
        ],
        name="finish",
    )(info, cov, upper, inv, low, *tiles)


AXES = ("row", "col")
PLACES = [(r, y, x, k) for r in range(8) for y in range(4) for x in range(4) for k in range(2)]


def place(r, y, x, k):
    return (r % 8) * 32 + (y % 4) * 8 + (x % 4) * 2 + k


def shift(value, source, dr=0, dy=0, dx=0, dk=0):
    pairs = [(place(*p), place(p[0] + dr, p[1] + dy, p[2] + dx, p[3] ^ dk)) for p in PLACES if source(*p)]
    return lax.ppermute(value, AXES, pairs)


def on_device(covariance):
    row = lax.axis_index("row")
    col = lax.axis_index("col")
    x, k = (col % 8) // 2, col % 2
    view = covariance.reshape(8, 256, 2, 2, 128).transpose(0, 1, 3, 2, 4).reshape(8, 1024, 128)
    panel = covariance[:, :, 0, :]
    upper = jnp.transpose(covariance[0], (1, 0, 2))

    head = lambda r, y, x, k: y == 0 and x == 0 and k == 0
    got = [shift(panel[2 * s:2 * s + 2], head, dx=s) for s in (1, 2, 3)]
    pair = got[0] + got[1] + got[2] + jnp.where(col == 0, panel[:2], 0.0)
    far = [shift(upper, lambda r, y, x, k: r == 0, dr=s) for s in (3, 5)]

    low, inv = chol_inverse(panel[0])
    inv = jnp.where((row == 0) & (col == 0), inv, 0.0)
    origin = lambda r, y, x, k: r == 0 and y == 0 and x == 0 and k == 0
    inv = sum([shift(inv, origin, dx=s) for s in (2, 1, 3)], inv)
    line = lambda r, y, x, k: r == 0 and y == 0 and k == 0
    inv = sum([shift(inv, line, dy=s) for s in (2, 1, 3)], inv)
    plane = lambda r, y, x, k: r == 0 and k == 0
    inv = sum([shift(inv, plane, dr=s) for s in (3, 5)], inv)
    inv = sum([shift(inv, lambda r, y, x, k: r in (0, 3, 5) and k == 0, dr=1),
               shift(inv, lambda r, y, x, k: r in (0, 3) and k == 0, dr=-1)], inv)
    inv = jnp.where(k == 0, inv, shift(inv, lambda r, y, x, k: True, dk=1))

    upper = jnp.where(row == 0, upper, far[0] + far[1])
    upper = upper + shift(upper, lambda r, y, x, k: r in (0, 3, 5), dr=1) + shift(upper, lambda r, y, x, k: r in (0, 3), dr=-1)

    other = shift(pair[1], lambda r, y, x, k: y == 0, dk=1)
    mine = jnp.where(k == 0, pair[0], other)
    front = lambda r, y, x, k: y == 0
    mine = sum([shift(mine, front, dy=s) for s in (2, 1, 3)], mine)
    whole = lambda r, y, x, k: True
    tiles = [mine] + [shift(mine, whole, dx=s) for s in (1, 2, 3)]
    tiles = tiles + [shift(t, whole, dk=1) for t in tiles]
    where_ = [2 * ((x - s) % 4) + kk for kk in (k, 1 - k) for s in range(4)]
    info = jnp.stack(where_ + [row, col]).astype(jnp.int32)
    out = finish(info, view, upper, inv, low, tiles)
    return out.reshape(8, 256, 2, 2, 128).transpose(0, 1, 3, 2, 4).reshape(8, 256, 2, 256)


def solution(mesh):
    return jax.shard_map(
        on_device,
        mesh=mesh,
        in_specs=(P(None, "row", None, "col"),),
        out_specs=P(None, "row", None, "col"),
        check_vma=False,
    )
```

```python
import jax
import jax.numpy as jnp
from jax import lax
from jax.experimental import pallas as pl
from jax.experimental.pallas import tpu as pltpu
from jax.sharding import PartitionSpec as P


HI = lax.Precision.HIGHEST


def dot(a, b, ca=1, cb=0, precision=HI):
    return lax.dot_general(a, b, (((ca,), (cb,)), ((), ())), precision=precision, preferred_element_type=jnp.float32)


def factor_block(block):
    n = block.shape[0]
    rows = lax.broadcasted_iota(jnp.int32, (n, n), 0)
    cols = lax.broadcasted_iota(jnp.int32, (n, n), 1)
    sub = lax.broadcasted_iota(jnp.int32, (8, n), 0)
    left = block
    right = jnp.where(rows == cols, 1.0, 0.0).astype(jnp.float32)
    inverse = []
    for g in range(n // 8):
        size = n - 8 * g
        for k in range(0, 8, 2):
            j = 8 * g + k
            c1 = jnp.broadcast_to(left[:, j:j + 1], (size, n))
            c2 = jnp.broadcast_to(left[:, j + 1:j + 2], (size, n))
            row1, row2 = left[k:k + 1, :], left[k + 1:k + 2, :]
            inv1, inv2 = right[k:k + 1, :], right[k + 1:k + 2, :]
            a = c1[k:k + 1]
            b = c2[k:k + 1]
            c = c2[k + 1:k + 2]
            ra = 1.0 / a
            m = b * ra
            d = c - b * m
            rd = 1.0 / d
            row2 = row2 - m * row1
            inv2 = inv2 - m * inv1
            v2, w2 = row2 * rd, inv2 * rd
            v1, w1 = row1 * ra - m * v2, inv1 * ra - m * w2
            sa, sd = lax.rsqrt(a), lax.rsqrt(d)
            inverse += [inv1 * sa, inv2 * sd]
            live = sub > k + 1
            t1 = jnp.where(live, c1[:8], 0.0)
            t2 = jnp.where(live, c2[:8], 0.0)
            if size > 8:
                c1 = jnp.concatenate([t1, c1[8:]], 0)
                c2 = jnp.concatenate([t2, c2[8:]], 0)
            else:
                c1, c2 = t1, t2
            left = left - c1 * v1 - c2 * v2
            right = right - c1 * w1 - c2 * w2
        left, right = left[8:], right[8:]
    return jnp.concatenate(inverse, 0)


def chol_kernel(a_ref, inv_ref):
    h = a_ref.shape[0] // 2
    chosen = (lax.axis_index("row") == 1) & (lax.axis_index("col") == 1)

    @pl.when(chosen)
    def _():
        y0 = factor_block(a_ref[:h, :h])
        l10 = dot(a_ref[h:, :h], y0, 1, 1)
        d1 = a_ref[h:, h:] - dot(l10, l10, 1, 1)
        y1 = factor_block(d1)
        mixed = -dot(y1, dot(l10, y0))
        inv_ref[:h, :h] = y0
        inv_ref[:h, h:] = y1
        inv_ref[h:, :h] = mixed[:h // 2]
        inv_ref[h:, h:] = mixed[h // 2:]

    @pl.when(jnp.logical_not(chosen))
    def _():
        inv_ref[...] = jnp.zeros(inv_ref.shape, jnp.float32)


VMEM = pl.BlockSpec(memory_space=pltpu.VMEM)
HBM = pl.BlockSpec(memory_space=pltpu.HBM)
ANY = pl.BlockSpec(memory_space=pl.ANY)
SMEM = pl.BlockSpec(memory_space=pltpu.SMEM)
PACKED = jax.ShapeDtypeStruct((192, 256), jnp.float32)
TILE = jax.ShapeDtypeStruct((256, 256), jnp.float32)
PAIR = jax.ShapeDtypeStruct((2, 256, 256), jnp.float32)


def chol_inverse(a):
    return pl.pallas_call(
        chol_kernel,
        out_shape=PACKED,
        in_specs=[VMEM],
        out_specs=VMEM,
        compiler_params=pltpu.CompilerParams(vmem_limit_bytes=8 * 2**20),
        name="chol",
    )(a)


def part(q, t):
    return pl.ds(2 * q + t, 256, stride=4)


def upper_kernel(cov_ref, corner_ref, upper_ref):
    for t in range(2):
        for q in range(2):
            value = cov_ref[part(q, t), :]
            upper_ref[t, :, 128 * q:128 * q + 128] = value
            if t == 0:
                corner_ref[:, 128 * q:128 * q + 128] = value


def take_upper(rows):
    return pl.pallas_call(
        upper_kernel,
        out_shape=(TILE, PAIR),
        in_specs=[VMEM],
        out_specs=(VMEM, VMEM),
        compiler_params=pltpu.CompilerParams(vmem_limit_bytes=8 * 2**20),
        name="take_upper",
    )(rows)


def panel_kernel(cov_ref, after_ref, *rest):
    outs, buf, sem = rest[:4], rest[4], rest[5]

    @pl.when(lax.axis_index("col") == 0)
    def _():
        for n in range(8):
            pltpu.make_async_copy(cov_ref.at[n], buf.at[n], sem.at[n]).start()
        for n in range(8):
            pltpu.make_async_copy(cov_ref.at[n], buf.at[n], sem.at[n]).wait()
            for q in range(2):
                outs[n // 2][n % 2, :, 128 * q:128 * q + 128] = buf[n, part(q, 0), :]


def take_panel(view, after):
    return pl.pallas_call(
        panel_kernel,
        out_shape=(PAIR,) * 4,
        in_specs=[HBM, ANY],
        out_specs=(VMEM,) * 4,
        scratch_shapes=[pltpu.VMEM((8, 1024, 128), jnp.float32), pltpu.SemaphoreType.DMA((8,))],
        compiler_params=pltpu.CompilerParams(vmem_limit_bytes=12 * 2**20),
        name="take_panel",
    )(view, after)


def pick(refs, j):
    return refs[j // 2].at[j % 2]


def final_kernel(cov_ref, upper_ref, inv0_ref, inv1_ref, *rest):
    own, got, out_ref = rest[:4], rest[4:8], rest[8]
    cov_buf, tile_buf, cov_sem, tile_sem, out_sem = rest[9:]
    row, col = lax.axis_index("row"), lax.axis_index("col")
    x, core = (col % 8) // 2, col % 2
    slot = [2 * ((x + s) % 4) + b for s, b in ((0, 0), (0, 1), (3, 0), (3, 1), (1, 0), (1, 1), (2, 0), (2, 1))]

    for j in range(8):
        pltpu.make_async_copy(cov_ref.at[slot[j]], cov_buf.at[j], cov_sem.at[j]).start()

        @pl.when(core == 0)
        def _():
            pltpu.make_async_copy(pick(own, j), tile_buf.at[j], tile_sem.at[j]).start()

        @pl.when(core == 1)
        def _():
            pltpu.make_async_copy(pick(got, j), tile_buf.at[j], tile_sem.at[j]).start()

    packed = jnp.where(core == 0, inv0_ref[...], inv1_ref[...])
    mixed = jnp.concatenate([packed[128:, :128], packed[128:, 128:]], 0)
    inv = jnp.concatenate([
        jnp.concatenate([packed[:128, :128], jnp.zeros((128, 128), jnp.float32)], 1),
        jnp.concatenate([mixed, packed[:128, 128:]], 1),
    ], 0)
    solved = [dot(inv, upper_ref[t]) for t in range(2)]
    weight = [dot(inv, solved[t], 0, 0) for t in range(2)]
    weight[0] = jnp.where(col == 0, -inv.T, weight[0])
    keep = jnp.where(col == 0, 0.0, 1.0).astype(jnp.float32)
    for j in range(8):
        pltpu.make_async_copy(pick(own, j), tile_buf.at[j], tile_sem.at[j]).wait()
        pltpu.make_async_copy(cov_ref.at[slot[j]], cov_buf.at[j], cov_sem.at[j]).wait()
        tile = tile_buf[j]
        for t in range(2):
            prod = dot(tile, weight[t])
            for q in range(2):
                old = cov_buf[j, part(q, t), :]
                if t == 0:
                    old = old * keep
                cov_buf[j, part(q, t), :] = old - prod[:, 128 * q:128 * q + 128]

        @pl.when((slot[j] == 0) & (row == 0))
        def _():
            rows = lax.broadcasted_iota(jnp.int32, (256, 256), 0)
            cols = lax.broadcasted_iota(jnp.int32, (256, 256), 1)
            factor = jnp.where(rows >= cols, solved[0].T, 0.0)
            first = jnp.where(col == 0, factor, solved[0])
            for t in range(2):
                for q in range(2):
                    new = (first if t == 0 else solved[t])[:, 128 * q:128 * q + 128]
                    cov_buf[j, part(q, t), :] = new

        pltpu.make_async_copy(cov_buf.at[j], out_ref.at[slot[j]], out_sem.at[j]).start()
    for j in range(8):
        pltpu.make_async_copy(cov_buf.at[j], out_ref.at[slot[j]], out_sem.at[j]).wait()


def finish(cov, upper, inv0, inv1, own, got):
    return pl.pallas_call(
        final_kernel,
        out_shape=jax.ShapeDtypeStruct(cov.shape, jnp.float32),
        in_specs=[HBM] + [VMEM] * 3 + [ANY] * 8,
        out_specs=HBM,
        scratch_shapes=[
            pltpu.VMEM((8, 1024, 128), jnp.float32),
            pltpu.VMEM((8, 256, 256), jnp.float32),
            pltpu.SemaphoreType.DMA((8,)),
            pltpu.SemaphoreType.DMA((8,)),
            pltpu.SemaphoreType.DMA((8,)),
        ],
        compiler_params=pltpu.CompilerParams(vmem_limit_bytes=16 * 2**20),
        name="finish",
    )(cov, upper, inv0, inv1, *own, *got)


AXES = ("row", "col")
PLACES = [(r, y, x, k) for r in range(8) for y in range(4) for x in range(4) for k in range(2)]


def place(r, y, x, k):
    return (r % 8) * 32 + (y % 4) * 8 + (x % 4) * 2 + k


def shift(value, source, dr=0, dy=0, dx=0, dk=0):
    pairs = [(place(*p), place(p[0] + dr, p[1] + dy, p[2] + dx, p[3] ^ dk)) for p in PLACES if source(*p)]
    return lax.ppermute(value, AXES, pairs)


def everyone(r, y, x, k):
    return True


def lane0(test):
    return lambda r, y, x, k: k == 0 and test(r, y, x)


def lane1(test):
    return lambda r, y, x, k: k == 1 and r == 1 and test(y, x)


def step(covariance):
    row = lax.axis_index("row")
    col = lax.axis_index("col")
    view = covariance.reshape(8, 256, 2, 2, 128).transpose(0, 1, 3, 2, 4).reshape(8, 1024, 128)

    corner, upper = take_upper(view[0])
    held = pltpu.with_memory_space_constraint(view, pltpu.HBM)
    panel = take_panel(held, corner)
    corner = shift(corner, lambda r, y, x, k: r == 0 and y == 0 and x == 0 and k == 0, dr=1, dk=1)
    far = [shift(upper, lambda r, y, x, k: r == 0, dr=s) for s in (3, 5)]
    inv = chol_inverse(corner)

    head = lane0(lambda r, y, x: y == 0 and x == 0)
    got = [shift(panel[s], head, dx=s) for s in (2, 1, 3)]
    pair = got[0] + got[1] + got[2] + jnp.where(col == 0, panel[0], 0.0)
    front = lane0(lambda r, y, x: y == 0)
    pair = sum([shift(pair, front, dy=s) for s in (2, 1, 3)], pair)
    full = lane0(lambda r, y, x: True)
    own = [pair] + [shift(pair, full, dx=s) for s in (1, 3, 2)]

    inv = sum([shift(inv, lane1(lambda y, x: y == 0 and x == 0), dx=s) for s in (2, 1, 3)], inv)
    inv = sum([shift(inv, lane1(lambda y, x: y == 0), dy=s) for s in (2, 1, 3)], inv)
    inv = sum([shift(inv, lane1(lambda y, x: True), dr=s) for s in (3, 5)], inv)
    inv = sum([shift(inv, lambda r, y, x, k: k == 1 and r in (1, 4, 6), dr=1),
               shift(inv, lambda r, y, x, k: k == 1 and r in (1, 4), dr=-1)], inv)

    upper = jnp.where(row == 0, upper, far[0] + far[1])
    near = [shift(upper, lambda r, y, x, k: r in (0, 3, 5), dr=1), shift(upper, lambda r, y, x, k: r in (0, 3), dr=-1)]
    upper = upper + near[0] + near[1]

    recv = [shift(s, everyone, dk=1) for s in own]
    inv0 = shift(inv, everyone, dk=1)
    out = finish(held, upper, inv0, inv, own, recv)
    return out.reshape(8, 256, 2, 2, 128).transpose(0, 1, 3, 2, 4).reshape(8, 256, 2, 256)


def solution(mesh):
    return jax.shard_map(
        step,
        mesh=mesh,
        in_specs=(P(None, "row", None, "col"),),
        out_specs=P(None, "row", None, "col"),
        check_vma=False,
    )
```
